256 devices in a mesh: dp: 8 (over z), expert: 8 (over y, core), mp: 4 (over x).
Axes of the slice: x: 4, y: 4, z: 8, core: 2. Of those that a mesh axis runs over, the one named last changes fastest.
Arguments:
- tokens: bfloat16 [8192, 2048], P(('dp', 'expert'), 'mp'), may hold values from -6 to 6
- targets: bfloat16 [8192, 2048], P(('dp', 'expert'), 'mp'), may hold values from -6 to 6
- token_weight: float32 [8192], P(('dp', 'expert')), may hold values from 0.5 to 11.7, as said below
- routes: int32 [8192, 2], P(('dp', 'expert')), may hold values from 0 to 7, all different within a row; in each aligned block of 128 rows (0 to 127, 128 to 255, ...) at most 40 rows name the same one
- router_weight: bfloat16 [2048, 8], P('mp'), may hold values from -0.125 to 0.125
- base_weight: bfloat16 [3, 8, 2048, 8192], P(None, 'expert', None, ('dp', 'mp')), may hold values from -0.125 to 0.125
- direction_one: bfloat16 [3, 8, 2048, 8192], P(None, 'expert', None, ('dp', 'mp')), may hold values from -0.125 to 0.125
- direction_two: bfloat16 [3, 8, 2048, 8192], P(None, 'expert', None, ('dp', 'mp')), may hold values from -0.125 to 0.125
- filter_scale: float32 [2, 8, 8192], P(None, 'expert', ('dp', 'mp')), may hold values from 0.5 to 2
- landscape: float32 [2], replicated, may hold values from -0.6 to 0.6
Outputs:
- mixed: bfloat16 [8192, 2048], P(('dp', 'expert'), 'mp')
- loss: float32 [1], replicated
The draws below stay inside these ranges and needn't reach their ends.
Inputs may be any that keep to these rules, and one draw needn't show every extreme that they name: `routes`: each row names 2 different experts. Within the rows of one group of dp and expert (aligned blocks of 128 rows) no expert is named more than 40 times, a bound that some block reaches. `token_weight`: Positive.
All inputs are finite; a program needn't handle non-finite values.
Results may differ from the reference program's by a relative error of at most 0.0028.
The reference program's roundings to bfloat16 on the way count: a program that leaves them out, or rounds other values in their place, can miss the bound.
Values may be sent and summed in bfloat16 or wider, within the bound.
No kernel may reach another device: no remote copies, remote signals or barrier semaphores. Data moves between devices by JAX's collectives and lax.ppermute only.
A program may use at most 128 MiB of HBM per device.

```python
import math
import jax
import jax.numpy as jnp
import numpy as np
from jax import lax

D = 2048
FF = 8192
E = 8
TOP = 2
TOK_DEV = 128
CAP = 40
TOKENS = 8192
N_DP = 8
N_EXPERT = 8


def draw_token_weight(key, part):
    position = jnp.arange(TOKENS, dtype=jnp.float32) / TOKENS
    ramp = 1.0 + 2.0 * position
    return ramp * jax.random.uniform(key, (TOKENS,), jnp.float32, 0.5, 1.5)


def shard_levels(stream_key, extent, split, least, top_value):
    factor_of, own = 1.0, jax.random.fold_in(stream_key, 6)
    for dim, shards_of in split:
        draws = jnp.exp(jax.random.uniform(jax.random.fold_in(own, dim), (shards_of,), jnp.float32, least / len(split), top_value / len(split)))
        factor_of = factor_of * jnp.repeat(draws, extent[dim] // shards_of).reshape([-1 if axis == dim else 1 for axis in range(len(extent))])
    return factor_of


def assign_block(own_key, own, number, rows, count, top, reach, skew):
    sequence = jax.random.permutation(own_key, count)
    heavy_load, ordinary = portions_of(count, rows * top, reach, skew, True), portions_of(count, rows * top, reach, skew, False)
    places = jnp.arange(count)

    def named(tallies, offset_by):
        used = int((tallies > 0).sum())
        fixed = max(1, used // 4)
        moved = fixed + (places - fixed + offset_by * (used - fixed)) % max(1, count - fixed)
        return jnp.zeros((count,), jnp.int32).at[sequence[jnp.where(places < fixed, places, moved)]].set(jnp.asarray(tallies, jnp.int32))

    tallies = jnp.where(number % 4 == 0, named(heavy_load, number // 4), named(ordinary, number - number // 4 - 1))
    mixed = jax.random.permutation(jax.random.fold_in(own, 3), count)
    donor, sink = mixed[0:count // 2 * 2:2], mixed[1:count // 2 * 2:2]
    slack = jnp.minimum(tallies[donor] - 1, reach - tallies[sink]) // 2
    slack = jnp.where((donor == sequence[0]) | (sink == sequence[0]) | (tallies[sink] == 0), 0, jnp.maximum(slack, 0))
    moved = jax.random.randint(jax.random.fold_in(own, 4), (count // 2,), 0, 1 << 20) % (slack + 1)
    tallies = tallies.at[donor].add(-moved).at[sink].add(moved)
    items = jnp.searchsorted(jnp.cumsum(tallies), jnp.arange(rows * top), side="right").astype(jnp.int32)
    listing = items.reshape(top, rows).T
    listing = listing[jax.random.permutation(jax.random.fold_in(own, 1), rows)]
    offset_by = jax.random.randint(jax.random.fold_in(own, 2), (rows, 1), 0, top)
    return jnp.take_along_axis(listing, (jnp.arange(top)[None, :] + offset_by) % top, axis=1)


def portions_of(amount, total, reach, lean, full):
    portions = [(1 << 20) // math.isqrt(rank ** lean) + 1 for rank in range(1, amount + 1)]
    largest = reach if full else min(reach, max(-(-total // amount), total * portions[0] // sum(portions)))
    least = 1 if total - largest >= amount - 1 else 0
    counts, spare = [largest] + [least] * (amount - 1), total - largest - least * (amount - 1)
    while spare > 0:
        free = [i for i in range(1, amount) if counts[i] < largest] or [i for i in range(1, amount) if counts[i] < reach]
        whole, remaining = sum([portions[i] for i in free]), spare
        for i in free:
            more = min(reach - counts[i], max(1, remaining * portions[i] // whole), spare)
            counts[i] = counts[i] + more
            spare = spare - more
    return np.array(counts)


def noise(rng, shape, width, limit, split=(), held_as=jnp.bfloat16):
    gain = shard_levels(rng, shape, split, -0.22, 0.18) if split else 1.0
    array = jax.random.normal(rng, shape, jnp.float32) * width * gain
    return jnp.minimum(jnp.maximum(array, -limit), limit).astype(held_as)


def setup_inputs(seed: int = 0) -> dict:
    key_of = jax.random.split(jax.random.key(seed), 11)
    tokens = noise(key_of[0], (TOKENS, D), 1.0, 6.0, ((0, 64), (1, 4)))
    targets = noise(key_of[1], (TOKENS, D), 1.0, 6.0, ((0, 64), (1, 4)))
    token_weight = draw_token_weight(jax.random.fold_in(key_of[10], 71), 0)
    routes_keys = jax.random.split(jax.random.fold_in(key_of[3], 1), TOKENS // TOK_DEV)
    routes_turns = jax.random.permutation(jax.random.fold_in(key_of[3], 3), TOKENS // TOK_DEV)
    routes = jax.vmap(lambda own, number: assign_block(jax.random.fold_in(key_of[3], 2), own, number, TOK_DEV, E, TOP, CAP, 2))(routes_keys, routes_turns).reshape((TOKENS, TOP))
    router_weight = noise(key_of[4], (D, E), D ** -0.5, 0.125, ((0, 4),))
    base_weight = noise(key_of[5], (3, E, D, FF), D ** -0.5, 0.125, ((1, 8), (3, 32)))
    direction_one = noise(key_of[6], (3, E, D, FF), D ** -0.5, 0.125, ((1, 8), (3, 32)))
    direction_two = noise(key_of[7], (3, E, D, FF), D ** -0.5, 0.125, ((1, 8), (3, 32)))
    filter_scale = jnp.clip(jnp.exp(math.log(2.0) - 1.3862944 * jax.random.uniform(key_of[8], (2, E, FF), jnp.float32) ** shard_levels(key_of[8], (2, E, FF), ((1, 8), (2, 32)), -0.2, 0.2)), 0.5, 2.0)
    landscape = jnp.clip(jax.random.uniform(key_of[9], (2,), jnp.float32, -0.6, 0.6), -0.6, 0.6)
    return dict(tokens=tokens, targets=targets, token_weight=token_weight, routes=routes, router_weight=router_weight, base_weight=base_weight, direction_one=direction_one, direction_two=direction_two, filter_scale=filter_scale, landscape=landscape)


def reference(tokens, targets, token_weight, routes, router_weight, base_weight, direction_one, direction_two, filter_scale, landscape):
    groups = N_DP * N_EXPERT
    logits = jnp.dot(tokens, router_weight, preferred_element_type=jnp.float32)
    expert_ids = jnp.arange(E, dtype=jnp.int32)
    pick_first = jnp.sum(jnp.where(routes[:, 0:1] == expert_ids[None, :], logits, jnp.float32(0.0)), axis=1)
    pick_second = jnp.sum(jnp.where(routes[:, 1:2] == expert_ids[None, :], logits, jnp.float32(0.0)), axis=1)
    gate_first = 1.0 / (1.0 + jnp.exp(pick_second - pick_first))
    gate_second = 1.0 / (1.0 + jnp.exp(pick_first - pick_second))
    grouped = routes.reshape(groups, TOK_DEV, 2)
    pair_ids = jnp.concatenate([grouped[:, :, 0], grouped[:, :, 1]], axis=1)
    onehot = (pair_ids[:, :, None] == expert_ids[None, None, :]).astype(jnp.int32)
    earlier = jnp.cumsum(onehot, axis=1) - onehot
    slot = jnp.sum(earlier * onehot, axis=2).astype(jnp.int32)
    flat_index = (pair_ids * CAP + slot).astype(jnp.int32)
    token_groups = tokens.reshape(groups, TOK_DEV, D)
    doubled = jnp.concatenate([token_groups, token_groups], axis=1)
    group_ids = jnp.arange(groups, dtype=jnp.int32)[:, None]
    buffer = jnp.zeros((groups, E * CAP, D), jnp.bfloat16).at[group_ids, flat_index].set(doubled)
    buffer = buffer.reshape(groups, E, CAP, D).transpose(1, 0, 2, 3)

    def run_expert(expert):
        slot_rows = lax.dynamic_index_in_dim(buffer, expert, 0, keepdims=False).reshape(groups * CAP, D)
        base_e = lax.dynamic_index_in_dim(base_weight, expert, 1, keepdims=False)
        one_e = lax.dynamic_index_in_dim(direction_one, expert, 1, keepdims=False)
        two_e = lax.dynamic_index_in_dim(direction_two, expert, 1, keepdims=False)
        scale_e = lax.dynamic_index_in_dim(filter_scale, expert, 1, keepdims=False)
        rebuilt = (base_e.astype(jnp.float32)
                   + landscape[0] * scale_e[0][None, None, :] * one_e.astype(jnp.float32)
                   + landscape[1] * scale_e[1][None, None, :] * two_e.astype(jnp.float32)).astype(jnp.bfloat16)
        gate_value = jnp.dot(slot_rows, rebuilt[0], preferred_element_type=jnp.float32)
        up_value = jnp.dot(slot_rows, rebuilt[1], preferred_element_type=jnp.float32)
        hidden = (jax.nn.silu(gate_value) * up_value).astype(jnp.bfloat16)
        result = jnp.dot(hidden, rebuilt[2].T, preferred_element_type=jnp.float32).astype(jnp.bfloat16)
        return result.reshape(groups, CAP, D)

    expert_out = lax.map(run_expert, jnp.arange(E, dtype=jnp.int32))
    out_flat = expert_out.transpose(1, 0, 2, 3).reshape(groups, E * CAP, D)
    picked = jnp.take_along_axis(out_flat, flat_index[:, :, None], axis=1).astype(jnp.float32)
    first_out = picked[:, :TOK_DEV].reshape(TOKENS, D)
    second_out = picked[:, TOK_DEV:].reshape(TOKENS, D)
    combined = tokens.astype(jnp.float32) + gate_first[:, None] * first_out + gate_second[:, None] * second_out
    error = combined - targets.astype(jnp.float32)
    loss = (jnp.sum(token_weight[:, None] * error * error) / (TOKENS * D)).reshape(1)
    return combined.astype(jnp.bfloat16), loss
```

```python
import jax
import jax.numpy as jnp
from jax import lax
from jax.sharding import Mesh
from jax.sharding import PartitionSpec as P

CAP = 40
EXPERT = ("expert_0", "expert_1")
DP_EXPERT = ("dp", "expert_0", "expert_1")
F32 = jnp.float32
BF16 = jnp.bfloat16
WIRE = jnp.float16


def shifted(array, axis, step):
    count = lax.axis_size(axis)
    return lax.ppermute(array, axis, [(i, (i + step) % count) for i in range(count)])


def summed(array, axis, combine):
    count = lax.axis_size(axis)
    step = 1
    while step < count:
        array = combine(array, shifted(array, axis, step))
        step *= 2
    return array


def rebuild(base_weight, direction_one, direction_two, filter_scale, landscape):
    scale_one = filter_scale[0][None, :]
    scale_two = filter_scale[1][None, :]
    merged = (
        base_weight.astype(F32)
        + landscape[0] * scale_one * direction_one.astype(F32)
        + landscape[1] * scale_two * direction_two.astype(F32)
    )
    return merged.astype(BF16)


def slot_target(routes, expert_count, capacity):
    pair_ids = jnp.concatenate([routes[:, 0], routes[:, 1]])
    expert_ids = jnp.arange(expert_count, dtype=jnp.int32)
    onehot = (pair_ids[:, None] == expert_ids[None, :]).astype(jnp.int32)
    earlier = jnp.cumsum(onehot, axis=0) - onehot
    slot = jnp.sum(earlier * onehot, axis=1)
    return pair_ids * capacity + slot


def per_device(
    tokens,
    targets,
    token_weight,
    routes,
    router_weight,
    base_weight,
    direction_one,
    direction_two,
    filter_scale,
    landscape,
):
    tok_rows, feat = tokens.shape
    expert_count = router_weight.shape[1]
    width = base_weight.shape[2]
    own_hidden = base_weight.shape[3]
    half_hidden = own_hidden // 2
    dp_count = lax.axis_size("dp")
    mp_count = lax.axis_size("mp")
    mp_index = lax.axis_index("mp")
    parity = lax.rem(mp_index, 2)

    with jax.named_scope("rebuild"):
        rebuilt = [
            rebuild(
                base_weight[m, 0], direction_one[m, 0], direction_two[m, 0],
                filter_scale[:, 0], landscape,
            )
            for m in range(3)
        ]
    even_pairs = [(0, 1), (1, 0), (2, 3), (3, 2)]
    odd_pairs = [(1, 2), (2, 1), (3, 0), (0, 3)]
    weights = []
    for matrix in rebuilt:
        first = lax.ppermute(matrix[:, :half_hidden], "mp", even_pairs)
        second = lax.ppermute(matrix[:, half_hidden:], "mp", odd_pairs)
        weights.append(jnp.concatenate([matrix, first, second], axis=1))
    gate_weight, up_weight, down_weight = weights

    flat_index = slot_target(routes, expert_count, CAP)
    placer = (
        flat_index[:, None] == jnp.arange(expert_count * CAP, dtype=jnp.int32)[None, :]
    ).astype(BF16)
    doubled = jnp.concatenate([tokens, tokens], axis=0)
    buffer = jnp.einsum("pk,pf->kf", placer, doubled, preferred_element_type=F32).astype(BF16)
    buffer = buffer.reshape(expert_count, CAP, feat)
    received = lax.all_to_all(buffer, EXPERT, split_axis=0, concat_axis=0, tiled=True)
    halves = received.reshape(2, (expert_count // 2) * CAP, feat)
    rows = halves.shape[1]
    part = rows // 2
    kept = lax.dynamic_index_in_dim(halves, parity, 0, keepdims=False)
    other = lax.dynamic_index_in_dim(halves, 1 - parity, 0, keepdims=False)
    pieces = {0: kept, 1: shifted(other, "mp", 1), 2: shifted(kept, "mp", 2), 3: shifted(other, "mp", 3)}
    slots = jnp.zeros((rows, width), BF16)
    for step, piece in pieces.items():
        source = lax.rem(mp_index - step + mp_count, mp_count)
        slots = lax.dynamic_update_slice(slots, piece, (0, source * feat))

    wide = [matrix.astype(F32) for matrix in rebuilt]
    energy = jnp.sum(jnp.sum(wide[0] ** 2, axis=0) * jnp.sum(wide[1] ** 2, axis=0))
    reach = jnp.max(jnp.sum(wide[2] ** 2, axis=1))
    longest = jnp.max(jnp.sum(slots.astype(F32) ** 2, axis=1))
    limits = jnp.stack([energy, reach, longest])
    limits = summed(summed(limits, "mp", jnp.maximum), "dp", jnp.maximum)
    devices = float(dp_count * mp_count)
    bound = 1.1 * devices * limits[2] * jnp.sqrt(limits[0]) * jnp.sqrt(limits[1])
    bound = jnp.maximum(bound, 1e-20)
    to_wire = 32768.0 / bound
    from_wire = bound * (1.0 / 32768.0)

    def expert(block):
        gate_value = jnp.dot(block, gate_weight, preferred_element_type=F32)
        up_value = jnp.dot(block, up_weight, preferred_element_type=F32)
        hidden = (jax.nn.silu(gate_value) * up_value).astype(BF16)
        return lax.dot_general(
            hidden, down_weight, (((1,), (1,)), ((), ())), preferred_element_type=F32
        )

    reach_steps = dp_count // 2
    own = [slots[:part], slots[part:]]
    forward = [own]
    backward = [own]
    for step in range(1, reach_steps + 1):
        last = step == reach_steps
        forward.append(
            [shifted(forward[-1][h], "dp", 1) if not (last and h == 1) else None for h in (0, 1)]
        )
        backward.append(
            [shifted(backward[-1][h], "dp", -1) if not (last and h == 0) else None for h in (0, 1)]
        )

    def partials(pair):
        out = expert(jnp.concatenate(pair, axis=0))
        return [out[:part] * to_wire, out[part:] * to_wire]

    own_out = partials(own)
    far_out = partials([forward[reach_steps][0], backward[reach_steps][1]])
    forward_out = [own_out] + [partials(forward[s]) for s in range(1, reach_steps)]
    backward_out = [own_out] + [partials(backward[s]) for s in range(1, reach_steps)]

    totals = []
    for half in (0, 1):
        near_first = half == 0
        back = far_out[0] if near_first else forward_out[reach_steps - 1][1]
        start = reach_steps if near_first else reach_steps - 1
        for step in range(start, 0, -1):
            arrived = shifted(back.astype(WIRE), "dp", -1).astype(F32)
            back = (forward_out[step - 1][half] if step > 1 else own_out[half]) + arrived
        ahead = far_out[1] if not near_first else backward_out[reach_steps - 1][0]
        start = reach_steps if not near_first else reach_steps - 1
        for step in range(start, 0, -1):
            arrived = shifted(ahead.astype(WIRE), "dp", 1).astype(F32)
            if step > 1:
                ahead = backward_out[step - 1][half] + arrived
            else:
                back = back + arrived
        totals.append(back)
    total = jnp.concatenate(totals, axis=0)

    def features_of(step):
        target = lax.rem(mp_index + step, mp_count)
        return lax.dynamic_slice(total, (0, target * feat), (rows, feat))

    far = shifted(features_of(2).astype(WIRE), "mp", 2).astype(F32)
    right = shifted(features_of(1).astype(WIRE), "mp", 1).astype(F32)
    left = shifted(features_of(3).astype(WIRE), "mp", 3).astype(F32)
    same = ((features_of(0) + far) * from_wire).astype(BF16)
    cross = ((right + left) * from_wire).astype(BF16)
    even = jnp.where(parity == 0, same, cross)
    odd = jnp.where(parity == 0, cross, same)
    expert_out = jnp.stack([even, odd]).reshape(expert_count, CAP, feat)
    returned = lax.all_to_all(expert_out, EXPERT, split_axis=0, concat_axis=0, tiled=True)

    partial_logits = jnp.dot(tokens, router_weight, preferred_element_type=F32)
    logits = summed(partial_logits, "mp", jnp.add)
    expert_ids = jnp.arange(expert_count, dtype=jnp.int32)
    pick_first = jnp.sum(jnp.where(routes[:, 0:1] == expert_ids[None, :], logits, 0.0), axis=1)
    pick_second = jnp.sum(jnp.where(routes[:, 1:2] == expert_ids[None, :], logits, 0.0), axis=1)
    gate_first = 1.0 / (1.0 + jnp.exp(pick_second - pick_first))
    gate_second = 1.0 / (1.0 + jnp.exp(pick_first - pick_second))

    out_rows = returned.reshape(expert_count * CAP, feat)
    first_out = jnp.take(out_rows, flat_index[:tok_rows], axis=0).astype(F32)
    second_out = jnp.take(out_rows, flat_index[tok_rows:], axis=0).astype(F32)
    combined = (
        tokens.astype(F32) + gate_first[:, None] * first_out + gate_second[:, None] * second_out
    )
    error = combined - targets.astype(F32)
    partial_loss = jnp.sum(token_weight[:, None] * error * error)
    loss_total = partial_loss
    for axis in ("expert_1", "mp", "expert_0", "dp"):
        loss_total = summed(loss_total.reshape(1, 1), axis, jnp.add)
    entries = tok_rows * dp_count * expert_count * feat * mp_count
    loss = (loss_total / entries).reshape(1)
    return (combined.astype(BF16), loss)


def solution(mesh):
    split = Mesh(
        mesh.devices.reshape(mesh.shape["dp"], 4, 2, mesh.shape["mp"]),
        ("dp", "expert_0", "expert_1", "mp"),
    )
    return jax.shard_map(
        per_device,
        mesh=split,
        in_specs=(
            P(DP_EXPERT, "mp"),
            P(DP_EXPERT, "mp"),
            P(DP_EXPERT),
            P(DP_EXPERT, None),
            P("mp", None),
            P(None, EXPERT, None, ("dp", "mp")),
            P(None, EXPERT, None, ("dp", "mp")),
            P(None, EXPERT, None, ("dp", "mp")),
            P(None, EXPERT, ("dp", "mp")),
            P(),
        ),
        out_specs=(P(DP_EXPERT, "mp"), P()),
        check_vma=False,
    )
```

```python
import jax
import jax.numpy as jnp
from jax import lax
from jax.experimental import pallas as pl
from jax.experimental.pallas import tpu as pltpu
from jax.sharding import Mesh
from jax.sharding import PartitionSpec as P

CAP = 40
EXPERT = ("expert_0", "expert_1")
DP_EXPERT = ("dp", "expert_0", "expert_1")
F32 = jnp.float32
BF16 = jnp.bfloat16
WIRE = jnp.float16


def shifted(array, axis, step):
    count = lax.axis_size(axis)
    return lax.ppermute(array, axis, [(i, (i + step) % count) for i in range(count)])


def to_all(array, axes):
    count = lax.axis_size(axes)
    copies = jnp.broadcast_to(array, (count, *array.shape))
    copies = lax.all_to_all(copies, axes, split_axis=0, concat_axis=0, tiled=True)
    return copies.reshape(count, *array.shape)[:, 0] if array.shape[0] == 1 else copies


def expert_kernel(*refs):
    units, refs = refs[:4], refs[4:]
    gate_ref, up_ref, down_ref, near, refs = refs[0], refs[1], refs[2], refs[3:9], refs[9:]
    scale_ref, outs, (slots, total) = refs[0], refs[1:5], refs[5:]
    part, width = units[0].shape
    hidden_count = gate_ref.shape[1]
    half = hidden_count // 2
    span = 512
    for i, unit in enumerate(units):
        slots[i * part : (i + 1) * part, :] = unit[...]
    scale = scale_ref[0]

    def product(weight):
        return jnp.dot(slots[...], weight, preferred_element_type=F32)

    def activated(gate_value, up_value):
        return (gate_value / (1.0 + jnp.exp(-gate_value)) * up_value).astype(BF16)

    own = activated(product(gate_ref[...]), product(up_ref[...]))
    first = activated(product(near[0][...]), product(near[2][...]))
    second = activated(product(near[1][...]), product(near[3][...]))

    def back(hidden, weight):
        return lax.dot_general(
            hidden, weight, (((1,), (1,)), ((), ())), preferred_element_type=F32
        )

    for block in range(width // span):
        cut = slice(block * span, (block + 1) * span)
        value = back(own, down_ref[cut, :]) + back(first, near[4][cut, :]) + back(second, near[5][cut, :])
        value = value * scale
        for i, out in enumerate(outs):
            out[:, cut] = value[i * part : (i + 1) * part]


def expert(units, rebuilt, neighbours, scale):
    part, width = units[0].shape
    hidden = 2 * rebuilt[0].shape[1]
    rows = len(units) * part
    near = [half for pair in neighbours for half in pair]
    whole = pl.BlockSpec(memory_space=pltpu.VMEM)
    return pl.pallas_call(
        expert_kernel,
        out_shape=[jax.ShapeDtypeStruct((part, width), F32)] * 4,
        in_specs=[whole] * 13 + [pl.BlockSpec(memory_space=pltpu.SMEM)],
        out_specs=[whole] * 4,
        scratch_shapes=[pltpu.VMEM((rows, width), BF16), pltpu.VMEM((8, 128), F32)],
        compiler_params=pltpu.CompilerParams(vmem_limit_bytes=40 * 1024 * 1024),
        cost_estimate=pl.CostEstimate(
            flops=6 * rows * width * hidden,
            bytes_accessed=6 * width * hidden + 6 * rows * width,
            transcendentals=rows * hidden,
        ),
    )(*units, *rebuilt, *near, scale.reshape(1))


def rebuild(base_weight, direction_one, direction_two, filter_scale, landscape):
    scale_one = filter_scale[0][None, :]
    scale_two = filter_scale[1][None, :]
    merged = (
        base_weight.astype(F32)
        + landscape[0] * scale_one * direction_one.astype(F32)
        + landscape[1] * scale_two * direction_two.astype(F32)
    )
    return merged.astype(BF16)


def slot_target(routes, expert_count, capacity):
    pair_ids = jnp.concatenate([routes[:, 0], routes[:, 1]])
    expert_ids = jnp.arange(expert_count, dtype=jnp.int32)
    onehot = (pair_ids[:, None] == expert_ids[None, :]).astype(jnp.int32)
    earlier = jnp.cumsum(onehot, axis=0) - onehot
    slot = jnp.sum(earlier * onehot, axis=1)
    return pair_ids * capacity + slot


def per_device(
    tokens,
    targets,
    token_weight,
    routes,
    router_weight,
    base_weight,
    direction_one,
    direction_two,
    filter_scale,
    landscape,
):
    tok_rows, feat = tokens.shape
    expert_count = router_weight.shape[1]
    width = base_weight.shape[2]
    own_hidden = base_weight.shape[3]
    half_hidden = own_hidden // 2
    dp_count = lax.axis_size("dp")
    mp_count = lax.axis_size("mp")
    mp_index = lax.axis_index("mp")
    parity = lax.rem(mp_index, 2)

    flat_index = slot_target(routes, expert_count, CAP)
    placer = (
        flat_index[:, None] == jnp.arange(expert_count * CAP, dtype=jnp.int32)[None, :]
    ).astype(BF16)
    doubled = jnp.concatenate([tokens, tokens], axis=0)
    buffer = jnp.einsum("pk,pf->kf", placer, doubled, preferred_element_type=F32).astype(BF16)
    buffer = buffer.reshape(expert_count, CAP, feat)
    received = lax.all_to_all(buffer, EXPERT, split_axis=0, concat_axis=0, tiled=True)
    halves = received.reshape(2, (expert_count // 2) * CAP, feat)
    rows = halves.shape[1]
    part = rows // 2
    kept = lax.dynamic_index_in_dim(halves, parity, 0, keepdims=False)
    other = lax.dynamic_index_in_dim(halves, 1 - parity, 0, keepdims=False)
    pieces = {0: kept, 1: shifted(other, "mp", 1), 2: shifted(kept, "mp", 2), 3: shifted(other, "mp", 3)}
    slots = jnp.zeros((rows, width), BF16)
    for step, piece in pieces.items():
        source = lax.rem(mp_index - step + mp_count, mp_count)
        slots = lax.dynamic_update_slice(slots, piece, (0, source * feat))

    with jax.named_scope("rebuild"):
        rebuilt = [
            rebuild(
                base_weight[m, 0], direction_one[m, 0], direction_two[m, 0],
                filter_scale[:, 0], landscape,
            )
            for m in range(3)
        ]
    even_pairs = [(0, 1), (1, 0), (2, 3), (3, 2)]
    odd_pairs = [(1, 2), (2, 1), (3, 0), (0, 3)]
    neighbours = []
    for matrix in rebuilt:
        first, second = matrix[:, :half_hidden], matrix[:, half_hidden:]
        first, second, _ = lax.optimization_barrier((first, second, pieces[2]))
        first = lax.ppermute(first, "mp", even_pairs)
        second = lax.ppermute(second, "mp", odd_pairs)
        neighbours.append((first, second))

    reach_steps = dp_count // 2
    own = [slots[:part], slots[part:]]
    forward = [own]
    backward = [own]
    for step in range(1, reach_steps + 1):
        last = step == reach_steps
        forward.append(
            [shifted(forward[-1][h], "dp", 1) if not (last and h == 1) else None for h in (0, 1)]
        )
        backward.append(
            [shifted(backward[-1][h], "dp", -1) if not (last and h == 0) else None for h in (0, 1)]
        )

    wide = [matrix.astype(F32) for matrix in rebuilt]
    energy = jnp.sum(jnp.sum(wide[0] ** 2, axis=0) * jnp.sum(wide[1] ** 2, axis=0))
    reach = jnp.max(jnp.sum(wide[2] ** 2, axis=1))
    longest = jnp.max(jnp.sum(received.astype(F32) ** 2, axis=2))
    limits = jnp.stack([energy, reach, longest])[None, :]
    limits, _ = lax.optimization_barrier((limits, forward[1][0]))
    limits = jnp.max(to_all(limits, ("dp", "mp")), axis=0)
    devices = float(dp_count * mp_count)
    bound = 1.1 * devices * mp_count * limits[2] * jnp.sqrt(limits[0]) * jnp.sqrt(limits[1])
    bound = jnp.maximum(bound, 1e-20)
    to_wire = 32768.0 / bound
    from_wire = bound * (1.0 / 32768.0)

    partial_logits = jnp.dot(tokens, router_weight, preferred_element_type=F32)
    partial_logits, _ = lax.optimization_barrier((partial_logits, forward[1][1]))
    logits = jnp.sum(to_all(partial_logits, "mp").reshape(mp_count, tok_rows, expert_count), axis=0)

    def partials(units, after):
        if after:
            units = lax.optimization_barrier((*units, *after))[: len(units)]
        return expert(units, rebuilt, neighbours, to_wire)

    outs = {}
    outs[1] = partials(forward[1] + backward[1], [forward[2][0], backward[2][1]])
    outs[2] = partials(forward[2] + backward[2], [forward[3][0], backward[3][1]])
    outs[3] = partials(forward[3] + backward[3], [])
    outs[4] = partials([forward[4][0], backward[4][1]] + own, [])
    own_out = outs[4][2:]
    far_out = outs[4][:2]
    forward_out = [own_out] + [outs[s][:2] for s in (1, 2, 3)]
    backward_out = [own_out] + [outs[s][2:] for s in (1, 2, 3)]

    totals = []
    for half in (0, 1):
        near_first = half == 0
        back = far_out[0] if near_first else forward_out[reach_steps - 1][1]
        start = reach_steps if near_first else reach_steps - 1
        for step in range(start, 0, -1):
            arrived = shifted(back.astype(WIRE), "dp", -1).astype(F32)
            back = (forward_out[step - 1][half] if step > 1 else own_out[half]) + arrived
        ahead = far_out[1] if not near_first else backward_out[reach_steps - 1][0]
        start = reach_steps if not near_first else reach_steps - 1
        for step in range(start, 0, -1):
            arrived = shifted(ahead.astype(WIRE), "dp", 1).astype(F32)
            if step > 1:
                ahead = backward_out[step - 1][half] + arrived
            else:
                back = back + arrived
        totals.append(back)
    total = jnp.concatenate(totals, axis=0)

    def features_of(step):
        target = lax.rem(mp_index + step, mp_count)
        return lax.dynamic_slice(total, (0, target * feat), (rows, feat))

    far = shifted(features_of(2).astype(WIRE), "mp", 2).astype(F32)
    right = shifted(features_of(1).astype(WIRE), "mp", 1).astype(F32)
    left = shifted(features_of(3).astype(WIRE), "mp", 3).astype(F32)
    same = ((features_of(0) + far) * from_wire).astype(BF16)
    cross = ((right + left) * from_wire).astype(BF16)
    even = jnp.where(parity == 0, same, cross)
    odd = jnp.where(parity == 0, cross, same)
    expert_out = jnp.stack([even, odd]).reshape(expert_count, CAP, feat)
    returned = lax.all_to_all(expert_out, EXPERT, split_axis=0, concat_axis=0, tiled=True)

    expert_ids = jnp.arange(expert_count, dtype=jnp.int32)
    pick_first = jnp.sum(jnp.where(routes[:, 0:1] == expert_ids[None, :], logits, 0.0), axis=1)
    pick_second = jnp.sum(jnp.where(routes[:, 1:2] == expert_ids[None, :], logits, 0.0), axis=1)
    gate_first = 1.0 / (1.0 + jnp.exp(pick_second - pick_first))
    gate_second = 1.0 / (1.0 + jnp.exp(pick_first - pick_second))

    out_rows = returned.reshape(expert_count * CAP, feat)
    first_out = jnp.take(out_rows, flat_index[:tok_rows], axis=0).astype(F32)
    second_out = jnp.take(out_rows, flat_index[tok_rows:], axis=0).astype(F32)
    combined = (
        tokens.astype(F32) + gate_first[:, None] * first_out + gate_second[:, None] * second_out
    )
    error = combined - targets.astype(F32)
    partial_loss = jnp.sum(token_weight[:, None] * error * error)
    loss_total = jnp.sum(to_all(partial_loss.reshape(1, 1), ("dp", "expert_0", "expert_1", "mp")))
    entries = tok_rows * dp_count * expert_count * feat * mp_count
    loss = (loss_total / entries).reshape(1)
    return (combined.astype(BF16), loss)


def solution(mesh):
    split = Mesh(
        mesh.devices.reshape(mesh.shape["dp"], 4, 2, mesh.shape["mp"]),
        ("dp", "expert_0", "expert_1", "mp"),
    )
    return jax.shard_map(
        per_device,
        mesh=split,
        in_specs=(
            P(DP_EXPERT, "mp"),
            P(DP_EXPERT, "mp"),
            P(DP_EXPERT),
            P(DP_EXPERT, None),
            P("mp", None),
            P(None, EXPERT, None, ("dp", "mp")),
            P(None, EXPERT, None, ("dp", "mp")),
            P(None, EXPERT, None, ("dp", "mp")),
            P(None, EXPERT, ("dp", "mp")),
            P(),
        ),
        out_specs=(P(DP_EXPERT, "mp"), P()),
        check_vma=False,
    )
```

```python
import functools

import jax
import jax.numpy as jnp
from jax import lax
from jax.experimental import pallas as pl
from jax.experimental.pallas import tpu as pltpu
from jax.sharding import Mesh
from jax.sharding import PartitionSpec as P

CAP = 40
MP = 4
EXPERT = ("expert_0", "expert_1")
DP_EXPERT = ("dp", "expert_0", "expert_1")
F32 = jnp.float32
BF16 = jnp.bfloat16
WIRE = jnp.float16


def shifted(array, axis, step):
    count = lax.axis_size(axis)
    return lax.ppermute(array, axis, [(i, (i + step) % count) for i in range(count)])


def to_all(array, axes):
    count = lax.axis_size(axes)
    copies = jnp.broadcast_to(array, (count, *array.shape))
    copies = lax.all_to_all(copies, axes, split_axis=0, concat_axis=0, tiled=True)
    return copies.reshape(count, *array.shape)


def expert_kernel(skips, index_ref, *refs):
    count = len(skips)
    blocks, weights, refs = refs[:count], refs[count : count + 6], refs[count + 6 :]
    outs, (slots,) = refs[:count], refs[count:]
    width = blocks[0].shape[1]
    feat = width // MP
    span = 512
    index = index_ref[0]
    row = 0
    for block, skip in zip(blocks, skips):
        rows = block.shape[0] - skip
        for step in range(MP):
            source = lax.rem(index + MP - step, MP)
            columns = pl.ds(pl.multiple_of(source * feat, feat), feat)
            slots[row : row + rows, columns] = block[skip:, step * feat : (step + 1) * feat]
        row += rows

    def hidden_of(gate, up):
        gate_value = jnp.dot(slots[...], gate[...], preferred_element_type=F32)
        up_value = jnp.dot(slots[...], up[...], preferred_element_type=F32)
        return (gate_value / (1.0 + jnp.exp(-gate_value)) * up_value).astype(BF16)

    own = hidden_of(weights[0], weights[1])
    near = hidden_of(weights[3], weights[4])

    def back(hidden, weight):
        return lax.dot_general(
            hidden, weight, (((1,), (1,)), ((), ())), preferred_element_type=F32
        )

    @pl.loop(0, width // span)
    def _(turn):
        cut = pl.ds(pl.multiple_of(turn * span, span), span)
        value = back(own, weights[2][cut, :]) + back(near, weights[5][cut, :])
        row = 0
        for out in outs:
            rows = out.shape[0]
            out[:, cut] = value[row : row + rows]
            row += rows


def expert(blocks, skips, own, near, index):
    width = blocks[0].shape[1]
    hidden = own[0].shape[1] + near[0].shape[1]
    count = len(blocks)
    heights = [block.shape[0] - skip for block, skip in zip(blocks, skips)]
    rows = sum(heights)
    whole = pl.BlockSpec(memory_space=pltpu.VMEM)
    return pl.pallas_call(
        functools.partial(expert_kernel, skips),
        out_shape=[jax.ShapeDtypeStruct((height, width), F32) for height in heights],
        in_specs=[pl.BlockSpec(memory_space=pltpu.SMEM)] + [whole] * (count + 6),
        out_specs=[whole] * count,
        scratch_shapes=[pltpu.VMEM((rows, width), BF16)],
        compiler_params=pltpu.CompilerParams(vmem_limit_bytes=40 * 1024 * 1024),
        cost_estimate=pl.CostEstimate(
            flops=6 * rows * width * hidden,
            bytes_accessed=6 * width * hidden + 6 * rows * width,
            transcendentals=rows * hidden,
        ),
    )(index, *blocks, *own, *near)


def rebuild(base_weight, direction_one, direction_two, filter_scale, landscape):
    scale_one = filter_scale[0][None, :, :]
    scale_two = filter_scale[1][None, :, :]
    merged = (
        base_weight[:, 0].astype(F32)
        + landscape[0] * scale_one * direction_one[:, 0].astype(F32)
        + landscape[1] * scale_two * direction_two[:, 0].astype(F32)
    )
    return merged.astype(BF16)


def slot_target(routes, expert_count, capacity):
    pair_ids = jnp.concatenate([routes[:, 0], routes[:, 1]])
    expert_ids = jnp.arange(expert_count, dtype=jnp.int32)
    onehot = (pair_ids[:, None] == expert_ids[None, :]).astype(jnp.int32)
    earlier = jnp.cumsum(onehot, axis=0) - onehot
    slot = jnp.sum(earlier * onehot, axis=1)
    return pair_ids * capacity + slot


def per_device(
    tokens,
    targets,
    token_weight,
    routes,
    router_weight,
    base_weight,
    direction_one,
    direction_two,
    filter_scale,
    landscape,
):
    tok_rows, feat = tokens.shape
    expert_count = router_weight.shape[1]
    width = base_weight.shape[2]
    own_hidden = base_weight.shape[3]
    half_hidden = own_hidden // 2
    dp_count = lax.axis_size("dp")
    mp_count = lax.axis_size("mp")
    mp_index = lax.axis_index("mp")
    parity = lax.rem(mp_index, 2)

    flat_index = slot_target(routes, expert_count, CAP)
    placer = (
        flat_index[:, None] == jnp.arange(expert_count * CAP, dtype=jnp.int32)[None, :]
    ).astype(BF16)
    doubled = jnp.concatenate([tokens, tokens], axis=0)
    buffer = jnp.einsum("pk,pf->kf", placer, doubled, preferred_element_type=F32).astype(BF16)
    buffer = buffer.reshape(expert_count, CAP, feat)
    received = lax.all_to_all(buffer, EXPERT, split_axis=0, concat_axis=0, tiled=True)
    halves = received.reshape(2, (expert_count // 2) * CAP, feat)
    rows = halves.shape[1]
    part = rows // 2

    rebuilt = rebuild(base_weight, direction_one, direction_two, filter_scale, landscape)
    own_weights = [rebuilt[m] for m in range(3)]

    partial_logits = lax.dot_general(
        router_weight, tokens, (((0,), (1,)), ((), ())), preferred_element_type=F32
    )
    high = lax.reduce_precision(partial_logits, 8, 7)
    middle = lax.reduce_precision(partial_logits - high, 8, 7)
    low = partial_logits - high - middle
    wide = [matrix.astype(F32) for matrix in own_weights]
    energy = jnp.sum(jnp.sum(wide[0] ** 2, axis=0) * jnp.sum(wide[1] ** 2, axis=0))
    reach = jnp.max(jnp.sum(wide[2] ** 2, axis=1))
    longest = jnp.max(jnp.sum(received.astype(F32) ** 2, axis=2))
    kind = lax.broadcasted_iota(jnp.int32, high.shape, 0)
    limits = 1.02 * jnp.where(kind == 0, energy, jnp.where(kind == 1, reach, longest))
    extra = jnp.concatenate([high, middle, low, limits], axis=1).astype(BF16)
    head = extra.shape[0]

    kept = lax.dynamic_index_in_dim(halves, parity, 0, keepdims=False)
    other = lax.dynamic_index_in_dim(halves, 1 - parity, 0, keepdims=False)
    kept = jnp.concatenate([extra, kept], axis=0)
    other = jnp.concatenate([extra, other], axis=0)
    pieces = [kept, shifted(other, "mp", 1), shifted(kept, "mp", 2), shifted(other, "mp", 3)]
    slots = jnp.concatenate(pieces, axis=1)

    first, second = rebuilt[:, :, :half_hidden], rebuilt[:, :, half_hidden:]
    first, second, _ = lax.optimization_barrier((first, second, pieces[2]))
    first = lax.ppermute(first, "mp", [(0, 1), (1, 0), (2, 3), (3, 2)])
    second = lax.ppermute(second, "mp", [(1, 2), (2, 1), (3, 0), (0, 3)])
    near_weights = [jnp.concatenate([first[m], second[m]], axis=1) for m in range(3)]
    place = mp_index.astype(jnp.int32).reshape(1)

    forward = [slots]
    backward = [slots]
    for step in range(1, dp_count // 2):
        forward.append(shifted(forward[-1], "dp", 1))
        backward.append(shifted(backward[-1], "dp", -1))
    far_low = shifted(forward[-1][: head + part], "dp", 1)
    far_high = shifted(backward[-1][head + part :], "dp", -1)

    heads = [block[:head] for block in forward + backward[1:] + [far_low]]
    limits = functools.reduce(jnp.maximum, [block.astype(F32) for block in heads])
    limits = jnp.max(limits.reshape(head, mp_count, feat)[:, :, feat - tok_rows :], axis=(1, 2))
    devices = float(dp_count * mp_count)
    bound = 1.1 * devices * mp_count * limits[2] * jnp.sqrt(limits[0]) * jnp.sqrt(limits[1])
    bound = jnp.maximum(bound, 1e-20)
    to_wire = 32768.0 / bound
    from_wire = bound * (1.0 / 32768.0)

    parts = slots[:head].astype(F32).reshape(head, mp_count, 4, tok_rows)[:, :, :3]
    logits = jnp.sum(parts, axis=(1, 2))

    def outputs(blocks, skips, after):
        blocks = lax.optimization_barrier((*blocks, *after))[: len(blocks)]
        return expert(blocks, skips, own_weights, near_weights, place)

    def wired(array):
        return (array * to_wire).astype(WIRE)

    def sent(array, step):
        return shifted(array, "dp", step).astype(F32)

    out_far = outputs([far_low, far_high], (head, 0), [])
    far_back, far_ahead = wired(out_far[0]), wired(out_far[1])
    out_one = outputs([forward[1], backward[1], slots], (head,) * 3, [forward[2], backward[2]])
    out_two = outputs([forward[2], backward[2]], (head,) * 2, [forward[3], backward[3]])
    out_three = outputs([forward[3], backward[3]], (head,) * 2, [far_back, far_ahead])
    own_out = out_one[2]

    back = sent(far_back, -1)
    ahead = sent(far_ahead, 1)
    below, above = out_three[0] * to_wire, out_three[1] * to_wire
    below = jnp.concatenate([below[:part] + back, below[part:]], axis=0).astype(WIRE)
    above = jnp.concatenate([above[:part], above[part:] + ahead], axis=0).astype(WIRE)
    back = sent(below, -1)
    ahead = sent(above, 1)
    for pair in (out_two, out_one):
        back = sent((pair[0] * to_wire + back).astype(WIRE), -1)
        ahead = sent((pair[1] * to_wire + ahead).astype(WIRE), 1)
    total = own_out * to_wire + back + ahead

    def features_of(step):
        target = lax.rem(mp_index + step, mp_count)
        return lax.dynamic_slice(total, (0, target * feat), (rows, feat))

    far = shifted(features_of(2).astype(WIRE), "mp", 2).astype(F32)
    right = shifted(features_of(1).astype(WIRE), "mp", 1).astype(F32)
    left = shifted(features_of(3).astype(WIRE), "mp", 3).astype(F32)
    same = ((features_of(0) + far) * from_wire).astype(BF16)
    cross = ((right + left) * from_wire).astype(BF16)
    even = jnp.where(parity == 0, same, cross)
    odd = jnp.where(parity == 0, cross, same)
    expert_out = jnp.stack([even, odd]).reshape(expert_count, CAP, feat)
    returned = lax.all_to_all(expert_out, EXPERT, split_axis=0, concat_axis=0, tiled=True)

    expert_ids = jnp.arange(expert_count, dtype=jnp.int32)
    pick_first = jnp.sum(jnp.where(routes[:, 0][None, :] == expert_ids[:, None], logits, 0.0), axis=0)
    pick_second = jnp.sum(jnp.where(routes[:, 1][None, :] == expert_ids[:, None], logits, 0.0), axis=0)
    gate_first = 1.0 / (1.0 + jnp.exp(pick_second - pick_first))
    gate_second = 1.0 / (1.0 + jnp.exp(pick_first - pick_second))

    out_rows = returned.reshape(expert_count * CAP, feat)
    first_out = jnp.take(out_rows, flat_index[:tok_rows], axis=0).astype(F32)
    second_out = jnp.take(out_rows, flat_index[tok_rows:], axis=0).astype(F32)
    combined = (
        tokens.astype(F32) + gate_first[:, None] * first_out + gate_second[:, None] * second_out
    )
    error = combined - targets.astype(F32)
    partial_loss = jnp.sum(token_weight[:, None] * error * error)
    loss_total = jnp.sum(to_all(partial_loss.reshape(1, 1), ("dp", "expert_0", "expert_1", "mp")))
    entries = tok_rows * dp_count * expert_count * feat * mp_count
    loss = (loss_total / entries).reshape(1)
    return (combined.astype(BF16), loss)


def solution(mesh):
    split = Mesh(
        mesh.devices.reshape(mesh.shape["dp"], 4, 2, mesh.shape["mp"]),
        ("dp", "expert_0", "expert_1", "mp"),
    )
    return jax.shard_map(
        per_device,
        mesh=split,
        in_specs=(
            P(DP_EXPERT, "mp"),
            P(DP_EXPERT, "mp"),
            P(DP_EXPERT),
            P(DP_EXPERT, None),
            P("mp", None),
            P(None, EXPERT, None, ("dp", "mp")),
            P(None, EXPERT, None, ("dp", "mp")),
            P(None, EXPERT, None, ("dp", "mp")),
            P(None, EXPERT, ("dp", "mp")),
            P(),
        ),
        out_specs=(P(DP_EXPERT, "mp"), P()),
        check_vma=False,
    )
```

```python
import functools

import jax
import jax.numpy as jnp
from jax import lax
from jax.experimental import pallas as pl
from jax.experimental.pallas import tpu as pltpu
from jax.sharding import Mesh
from jax.sharding import PartitionSpec as P

CAP = 40
MP = 4
EXPERT = ("expert_0", "expert_1")
DP_EXPERT = ("dp", "expert_0", "expert_1")
F32 = jnp.float32
BF16 = jnp.bfloat16
WIRE = jnp.float16


def shifted(array, axis, step):
    count = lax.axis_size(axis)
    return lax.ppermute(array, axis, [(i, (i + step) % count) for i in range(count)])


def to_all(array, axes):
    count = lax.axis_size(axes)
    copies = jnp.broadcast_to(array, (count, *array.shape))
    copies = lax.all_to_all(copies, axes, split_axis=0, concat_axis=0, tiled=True)
    return copies.reshape(count, *array.shape)


def hidden_of(slots, rows, weights):
    hidden = []
    for gate, up, _ in weights:
        gate_value = jnp.dot(slots[rows, :], gate[...], preferred_element_type=F32)
        up_value = jnp.dot(slots[rows, :], up[...], preferred_element_type=F32)
        hidden.append((gate_value / (1.0 + jnp.exp(-gate_value)) * up_value).astype(BF16))
    return hidden


def output_of(value, hidden, weights, width, start, span):
    for values, (_, _, downs) in zip(hidden, weights):
        depth = width // len(downs)
        down = downs[start // depth]
        first = start % depth
        added = lax.dot_general(
            values, down[first : first + span, :], (((1,), (1,)), ((), ())),
            preferred_element_type=F32,
        )
        value = added if value is None else value + added
    return value


def first_kernel(skips, index_ref, *refs):
    count = len(skips)
    blocks, (gate, up, down, slots, total) = refs[:count], refs[count:]
    feat = slots.shape[1] // MP
    index = index_ref[0]
    row = 0
    for block, skip in zip(blocks, skips):
        rows = block.shape[0] - skip
        for step in range(MP):
            source = lax.rem(index + MP - step, MP)
            columns = pl.ds(pl.multiple_of(source * feat, feat), feat)
            slots[row : row + rows, columns] = block[skip:, step * feat : (step + 1) * feat]
        row += rows
    pass_through(slots, None, total, [(gate, up, (down,))])


def pass_through(slots, before, total, weights):
    height, width = slots.shape
    chunk = height // 2
    span = 512

    @pl.loop(0, 2)
    def _(turn):
        rows = pl.ds(pl.multiple_of(turn * chunk, chunk), chunk)
        hidden = hidden_of(slots, rows, weights)
        for start in range(0, width, span):
            cut = slice(start, start + span)
            value = None if before is None else before[rows, cut]
            total[rows, cut] = output_of(value, hidden, weights, width, start, span)


def middle_kernel(slots, before, *refs):
    weights, total = refs[:-1], refs[-1]
    sets = [(weights[i], weights[i + 1], weights[i + 2 : i + 3]) for i in range(0, len(weights), 3)]
    pass_through(slots, before, total, sets)


def last_kernel(slots, before, gate, up, low, high, *outs):
    height, width = slots.shape
    chunk = height // 2
    span = 512
    weights = [(gate, up, (low, high))]
    for turn in (1, 0):
        rows = slice(turn * chunk, (turn + 1) * chunk)
        hidden = hidden_of(slots, rows, weights)
        for start in range(0, width, span):
            cut = slice(start, start + span)
            value = output_of(before[rows, cut], hidden, weights, width, start, span)
            row = 0
            for out in outs:
                size = out.shape[0]
                if turn * chunk <= row < (turn + 1) * chunk:
                    at = row - turn * chunk
                    out[:, cut] = value[at : at + size]
                row += size


def expert_call(kernel, args, out_shape, rows, width, hidden, scalars):
    whole = pl.BlockSpec(memory_space=pltpu.VMEM)
    single = isinstance(out_shape, jax.ShapeDtypeStruct)
    return pl.pallas_call(
        kernel,
        out_shape=out_shape,
        in_specs=[pl.BlockSpec(memory_space=pltpu.SMEM)] * scalars + [whole] * (len(args) - scalars),
        out_specs=whole if single else [whole] * len(out_shape),
        compiler_params=pltpu.CompilerParams(vmem_limit_bytes=44 * 1024 * 1024),
        cost_estimate=pl.CostEstimate(
            flops=6 * rows * width * hidden,
            bytes_accessed=6 * width * hidden + 8 * rows * width,
            transcendentals=rows * hidden,
        ),
    )(*args)


def rebuild(base_weight, direction_one, direction_two, filter_scale, landscape):
    scale_one = filter_scale[0][None, :]
    scale_two = filter_scale[1][None, :]
    merged = (
        base_weight.astype(F32)
        + landscape[0] * scale_one * direction_one.astype(F32)
        + landscape[1] * scale_two * direction_two.astype(F32)
    )
    return merged.astype(BF16)


def rebuild_kernel(landscape_ref, base_ref, one_ref, two_ref, scale_ref, out_ref):
    scale_one = landscape_ref[0] * scale_ref[0]
    scale_two = landscape_ref[1] * scale_ref[1]
    merged = (
        base_ref[0, 0].astype(F32)
        + scale_one * one_ref[0, 0].astype(F32)
        + scale_two * two_ref[0, 0].astype(F32)
    )
    out_ref[...] = merged.astype(BF16)


def rebuild_call(matrix, base_weight, direction_one, direction_two, filter_scale, landscape):
    _, _, width, hidden = base_weight.shape
    rows = width // 4
    block = pl.BlockSpec((1, 1, rows, hidden), lambda i: (matrix, 0, i, 0))
    return pl.pallas_call(
        rebuild_kernel,
        grid=(width // rows,),
        out_shape=jax.ShapeDtypeStruct((width, hidden), BF16),
        in_specs=[
            pl.BlockSpec(memory_space=pltpu.SMEM),
            block,
            block,
            block,
            pl.BlockSpec(filter_scale.shape, lambda i: (0, 0, 0)),
        ],
        out_specs=pl.BlockSpec((rows, hidden), lambda i: (i, 0)),
        compiler_params=pltpu.CompilerParams(vmem_limit_bytes=62 * 1024 * 1024),
        cost_estimate=pl.CostEstimate(
            flops=4 * width * hidden, bytes_accessed=8 * width * hidden, transcendentals=0
        ),
    )(landscape, base_weight, direction_one, direction_two, filter_scale)


def slot_target(routes, expert_count, capacity):
    pair_ids = jnp.concatenate([routes[:, 0], routes[:, 1]])
    expert_ids = jnp.arange(expert_count, dtype=jnp.int32)
    onehot = (pair_ids[:, None] == expert_ids[None, :]).astype(jnp.int32)
    earlier = jnp.cumsum(onehot, axis=0) - onehot
    slot = jnp.sum(earlier * onehot, axis=1)
    return pair_ids * capacity + slot


def per_device(
    tokens,
    targets,
    token_weight,
    routes,
    router_weight,
    base_weight,
    direction_one,
    direction_two,
    filter_scale,
    landscape,
):
    tok_rows, feat = tokens.shape
    expert_count = router_weight.shape[1]
    width = base_weight.shape[2]
    own_hidden = base_weight.shape[3]
    dp_count = lax.axis_size("dp")
    mp_count = lax.axis_size("mp")
    mp_index = lax.axis_index("mp")

    def rebuilt(m, scale):
        return rebuild(base_weight[m, 0], direction_one[m, 0], direction_two[m, 0], scale[:, 0], landscape)

    gate_own = rebuild_call(0, base_weight, direction_one, direction_two, filter_scale, landscape)
    gate_left = shifted(gate_own, "mp", 1)
    gate_right = shifted(gate_own, "mp", -1)
    tokens_then, _ = lax.optimization_barrier((tokens, gate_own))

    flat_index = slot_target(routes, expert_count, CAP)
    placer = (
        flat_index[:, None] == jnp.arange(expert_count * CAP, dtype=jnp.int32)[None, :]
    ).astype(BF16)
    doubled = jnp.concatenate([tokens_then, tokens_then], axis=0)
    buffer = jnp.einsum("pk,pf->kf", placer, doubled, preferred_element_type=F32).astype(BF16)
    buffer = buffer.reshape(expert_count, CAP, feat)
    received = lax.all_to_all(buffer, EXPERT, split_axis=0, concat_axis=0, tiled=True)
    quarters = received.reshape(mp_count, (expert_count // mp_count) * CAP, feat)
    rows = quarters.shape[1]
    part = rows // 2

    scale_then, _ = lax.optimization_barrier((filter_scale, buffer))
    up_own, down_own = rebuilt(1, scale_then), rebuilt(2, scale_then)

    partial_logits = lax.dot_general(
        router_weight, tokens, (((0,), (1,)), ((), ())), preferred_element_type=F32
    )
    high = lax.reduce_precision(partial_logits, 8, 7)
    middle = lax.reduce_precision(partial_logits - high, 8, 7)
    low = partial_logits - high - middle
    wide = [matrix.astype(F32) for matrix in (gate_own, up_own, down_own)]
    energy = jnp.sum(jnp.sum(wide[0] ** 2, axis=0) * jnp.sum(wide[1] ** 2, axis=0))
    reach = jnp.max(jnp.sum(wide[2] ** 2, axis=1))
    longest = jnp.max(jnp.sum(received.astype(F32) ** 2, axis=2))
    kind = lax.broadcasted_iota(jnp.int32, high.shape, 0)
    limits = 1.02 * jnp.where(kind == 0, energy, jnp.where(kind == 1, reach, longest))
    extra = jnp.concatenate([high, middle, low, limits], axis=1).astype(BF16)
    head = extra.shape[0]

    pieces = []
    for step in range(mp_count):
        target = lax.rem(mp_index + step, mp_count)
        piece = lax.dynamic_index_in_dim(quarters, target, 0, keepdims=False)
        piece = jnp.concatenate([extra, piece], axis=0)
        pieces.append(shifted(piece, "mp", step) if step else piece)
    slots = jnp.concatenate(pieces, axis=1)

    up_then, down_then, _ = lax.optimization_barrier((up_own, down_own, received))
    up_left = shifted(up_then, "mp", 1)
    up_right = shifted(up_then, "mp", -1)
    down_left = shifted(down_then, "mp", 1)
    down_right = shifted(down_then, "mp", -1)
    gate_far = shifted(gate_left, "mp", 1)
    up_far = shifted(up_right, "mp", -1)

    forward = [slots]
    backward = [slots]
    for _ in range(1, dp_count // 2):
        forward.append(shifted(forward[-1], "dp", 1))
        backward.append(shifted(backward[-1], "dp", -1))
    far_low = shifted(forward[-1][: head + part], "dp", 1)
    far_high = shifted(backward[-1][head + part :], "dp", -1)

    middle_row = width // 2
    first_half, second_half, _, _ = lax.optimization_barrier((down_left, down_right, far_low, far_high))
    down_far = (
        shifted(first_half[:middle_row], "mp", 1), shifted(second_half[middle_row:], "mp", -1)
    )

    heads = [block[:head] for block in forward + backward[1:] + [far_low]]
    limits = functools.reduce(jnp.maximum, [block.astype(F32) for block in heads])
    limits = jnp.max(limits.reshape(head, mp_count, feat)[:, :, feat - tok_rows :], axis=(1, 2))
    devices = float(dp_count * mp_count)
    bound = 1.1 * devices * mp_count * limits[2] * jnp.sqrt(limits[0]) * jnp.sqrt(limits[1])
    bound = jnp.maximum(bound, 1e-20)
    to_wire = 32768.0 / bound
    from_wire = bound * (1.0 / 32768.0)

    parts = slots[:head].astype(F32).reshape(head, mp_count, 4, tok_rows)[:, :, :3]
    logits = jnp.sum(parts, axis=(1, 2))

    blocks = [slots]
    for ahead, behind in zip(forward[1:], backward[1:]):
        blocks += [ahead, behind]
    blocks += [far_low, far_high]
    skips = (head,) * (len(blocks) - 1) + (0,)
    all_rows = dp_count * rows
    slots_shape = jax.ShapeDtypeStruct((all_rows, width), BF16)
    total_shape = jax.ShapeDtypeStruct((all_rows, width), F32)
    place = mp_index.astype(jnp.int32).reshape(1)
    every, sums = expert_call(
        functools.partial(first_kernel, skips),
        (place, *blocks, gate_own, up_own, down_own),
        [slots_shape, total_shape], all_rows, width, own_hidden, 1,
    )
    sums = expert_call(
        middle_kernel,
        (every, sums, gate_left, up_left, down_left, gate_right, up_right, down_right),
        total_shape, all_rows, width, 2 * own_hidden, 0,
    )
    heights = [rows] * (dp_count - 1) + [part, part]
    outs = expert_call(
        last_kernel,
        (every, sums, gate_far, up_far, *down_far),
        [jax.ShapeDtypeStruct((height, width), F32) for height in heights],
        all_rows, width, own_hidden, 0,
    )
    outs = [out * to_wire for out in outs]

    def both(below, above):
        pair = lax.optimization_barrier((below.astype(WIRE), above.astype(WIRE)))
        pair = lax.optimization_barrier((shifted(pair[0], "dp", -1), shifted(pair[1], "dp", 1)))
        return pair[0].astype(F32), pair[1].astype(F32)

    back, ahead = both(outs[-2], outs[-1])
    below, above = outs[-4], outs[-3]
    below = jnp.concatenate([below[:part] + back, below[part:]], axis=0)
    above = jnp.concatenate([above[:part], above[part:] + ahead], axis=0)
    back, ahead = both(below, above)
    for step in range(dp_count // 2 - 2, 0, -1):
        back, ahead = both(outs[2 * step - 1] + back, outs[2 * step] + ahead)
    result = ((outs[0] + back + ahead) * from_wire).astype(BF16)

    arrived = []
    for step in range(mp_count):
        target = lax.rem(mp_index + step, mp_count)
        piece = lax.dynamic_slice(result, (0, target * feat), (rows, feat))
        arrived.append(shifted(piece, "mp", step) if step else piece)

    def quarter(place):
        step = lax.rem(mp_index - place + mp_count, mp_count)
        chosen = arrived[-1]
        for i, piece in enumerate(arrived[:-1]):
            chosen = jnp.where(step == i, piece, chosen)
        return chosen

    expert_out = jnp.stack([quarter(i) for i in range(mp_count)]).reshape(expert_count, CAP, feat)
    returned = lax.all_to_all(expert_out, EXPERT, split_axis=0, concat_axis=0, tiled=True)

    expert_ids = jnp.arange(expert_count, dtype=jnp.int32)
    pick_first = jnp.sum(jnp.where(routes[:, 0][None, :] == expert_ids[:, None], logits, 0.0), axis=0)
    pick_second = jnp.sum(jnp.where(routes[:, 1][None, :] == expert_ids[:, None], logits, 0.0), axis=0)
    gate_first = 1.0 / (1.0 + jnp.exp(pick_second - pick_first))
    gate_second = 1.0 / (1.0 + jnp.exp(pick_first - pick_second))

    out_rows = returned.reshape(expert_count * CAP, feat)
    picked = jnp.dot(placer, out_rows, preferred_element_type=F32)
    first_out, second_out = picked[:tok_rows], picked[tok_rows:]
    combined = (
        tokens.astype(F32) + gate_first[:, None] * first_out + gate_second[:, None] * second_out
    )
    error = combined - targets.astype(F32)
    partial_loss = jnp.sum(token_weight[:, None] * error * error)
    loss_total = jnp.sum(to_all(partial_loss.reshape(1, 1), ("dp", "expert_0", "expert_1", "mp")))
    entries = tok_rows * dp_count * expert_count * feat * mp_count
    loss = (loss_total / entries).reshape(1)
    return (combined.astype(BF16), loss)


def solution(mesh):
    split = Mesh(
        mesh.devices.reshape(mesh.shape["dp"], 4, 2, mesh.shape["mp"]),
        ("dp", "expert_0", "expert_1", "mp"),
    )

    return jax.shard_map(
        per_device,
        mesh=split,
        in_specs=(
            P(DP_EXPERT, "mp"),
            P(DP_EXPERT, "mp"),
            P(DP_EXPERT),
            P(DP_EXPERT, None),
            P("mp", None),
            P(None, EXPERT, None, ("dp", "mp")),
            P(None, EXPERT, None, ("dp", "mp")),
            P(None, EXPERT, None, ("dp", "mp")),
            P(None, EXPERT, ("dp", "mp")),
            P(),
        ),
        out_specs=(P(DP_EXPERT, "mp"), P()),
        check_vma=False,
    )
```

```python
import functools

import jax
import jax.numpy as jnp
from jax import lax
from jax.experimental import pallas as pl
from jax.experimental.pallas import tpu as pltpu
from jax.sharding import Mesh
from jax.sharding import PartitionSpec as P

CAP = 40
MP = 4
EXPERT = ("expert_0", "expert_1")
DP_EXPERT = ("dp", "expert_0", "expert_1")
F32 = jnp.float32
BF16 = jnp.bfloat16
WIRE = jnp.float16


def shifted(array, axis, step):
    count = lax.axis_size(axis)
    return lax.ppermute(array, axis, [(i, (i + step) % count) for i in range(count)])


def to_all(array, axes):
    count = lax.axis_size(axes)
    copies = jnp.broadcast_to(array, (count, *array.shape))
    copies = lax.all_to_all(copies, axes, split_axis=0, concat_axis=0, tiled=True)
    return copies.reshape(count, *array.shape)


def hidden_of(slots, rows, weights):
    hidden = []
    for gate, up, _ in weights:
        gate_value = jnp.dot(slots[rows, :], gate[...], preferred_element_type=F32)
        up_value = jnp.dot(slots[rows, :], up[...], preferred_element_type=F32)
        hidden.append((gate_value / (1.0 + jnp.exp(-gate_value)) * up_value).astype(BF16))
    return hidden


def output_of(value, hidden, weights, width, start, span):
    for values, (_, _, downs) in zip(hidden, weights):
        depth = width // len(downs)
        down = downs[start // depth]
        first = start % depth
        added = lax.dot_general(
            values, down[first : first + span, :], (((1,), (1,)), ((), ())),
            preferred_element_type=F32,
        )
        value = added if value is None else value + added
    return value


def first_kernel(skips, index_ref, *refs):
    count = len(skips)
    blocks, (gate, up, down, slots, total) = refs[:count], refs[count:]
    feat = slots.shape[1] // MP
    index = index_ref[0]
    row = 0
    for block, skip in zip(blocks, skips):
        rows = block.shape[0] - skip
        for step in range(MP):
            source = lax.rem(index + MP - step, MP)
            columns = pl.ds(pl.multiple_of(source * feat, feat), feat)
            slots[row : row + rows, columns] = block[skip:, step * feat : (step + 1) * feat]
        row += rows
    pass_through(slots, None, total, [(gate, up, (down,))])


def pass_through(slots, before, total, weights):
    height, width = slots.shape
    chunk = height // 2
    span = 512

    @pl.loop(0, 2)
    def _(turn):
        rows = pl.ds(pl.multiple_of(turn * chunk, chunk), chunk)
        hidden = hidden_of(slots, rows, weights)
        for start in range(0, width, span):
            cut = slice(start, start + span)
            value = None if before is None else before[rows, cut]
            total[rows, cut] = output_of(value, hidden, weights, width, start, span)


def middle_kernel(slots, before, *refs):
    weights, total = refs[:-1], refs[-1]
    sets = [(weights[i], weights[i + 1], weights[i + 2 : i + 3]) for i in range(0, len(weights), 3)]
    pass_through(slots, before, total, sets)


def hidden_kernel(slots, gate, up, out):
    chunk = slots.shape[0] // 2

    @pl.loop(0, 2)
    def _(turn):
        rows = pl.ds(pl.multiple_of(turn * chunk, chunk), chunk)
        out[rows, :] = hidden_of(slots, rows, [(gate, up, None)])[0]


def last_kernel(values, before, low, high, *outs):
    height, width = before.shape
    chunk = height // 2
    span = 512
    weights = [(None, None, (low, high))]
    for turn in (1, 0):
        rows = slice(turn * chunk, (turn + 1) * chunk)
        hidden = [values[rows, :]]
        for start in range(0, width, span):
            cut = slice(start, start + span)
            value = output_of(before[rows, cut], hidden, weights, width, start, span)
            row = 0
            for out in outs:
                size = out.shape[0]
                if turn * chunk <= row < (turn + 1) * chunk:
                    at = row - turn * chunk
                    out[:, cut] = value[at : at + size]
                row += size


def expert_call(kernel, args, out_shape, rows, width, hidden, scalars):
    whole = pl.BlockSpec(memory_space=pltpu.VMEM)
    single = isinstance(out_shape, jax.ShapeDtypeStruct)
    return pl.pallas_call(
        kernel,
        out_shape=out_shape,
        in_specs=[pl.BlockSpec(memory_space=pltpu.SMEM)] * scalars + [whole] * (len(args) - scalars),
        out_specs=whole if single else [whole] * len(out_shape),
        compiler_params=pltpu.CompilerParams(vmem_limit_bytes=44 * 1024 * 1024),
        cost_estimate=pl.CostEstimate(
            flops=6 * rows * width * hidden,
            bytes_accessed=6 * width * hidden + 8 * rows * width,
            transcendentals=rows * hidden,
        ),
    )(*args)


def rebuild(base_weight, direction_one, direction_two, filter_scale, landscape):
    scale_one = filter_scale[0][None, :]
    scale_two = filter_scale[1][None, :]
    merged = (
        base_weight.astype(F32)
        + landscape[0] * scale_one * direction_one.astype(F32)
        + landscape[1] * scale_two * direction_two.astype(F32)
    )
    return merged.astype(BF16)


def rebuild_kernel(landscape_ref, base_ref, one_ref, two_ref, scale_ref, out_ref):
    scale_one = landscape_ref[0] * scale_ref[0]
    scale_two = landscape_ref[1] * scale_ref[1]
    merged = (
        base_ref[0, 0].astype(F32)
        + scale_one * one_ref[0, 0].astype(F32)
        + scale_two * two_ref[0, 0].astype(F32)
    )
    out_ref[...] = merged.astype(BF16)


def rebuild_call(matrix, base_weight, direction_one, direction_two, filter_scale, landscape):
    _, _, width, hidden = base_weight.shape
    rows = width // 4
    block = pl.BlockSpec((1, 1, rows, hidden), lambda i: (matrix, 0, i, 0))
    return pl.pallas_call(
        rebuild_kernel,
        grid=(width // rows,),
        out_shape=jax.ShapeDtypeStruct((width, hidden), BF16),
        in_specs=[
            pl.BlockSpec(memory_space=pltpu.SMEM),
            block,
            block,
            block,
            pl.BlockSpec(filter_scale.shape, lambda i: (0, 0, 0)),
        ],
        out_specs=pl.BlockSpec((rows, hidden), lambda i: (i, 0)),
        compiler_params=pltpu.CompilerParams(vmem_limit_bytes=62 * 1024 * 1024),
        cost_estimate=pl.CostEstimate(
            flops=4 * width * hidden, bytes_accessed=8 * width * hidden, transcendentals=0
        ),
    )(landscape, base_weight, direction_one, direction_two, filter_scale)


def slot_target(routes, expert_count, capacity):
    pair_ids = jnp.concatenate([routes[:, 0], routes[:, 1]])
    expert_ids = jnp.arange(expert_count, dtype=jnp.int32)
    onehot = (pair_ids[:, None] == expert_ids[None, :]).astype(jnp.int32)
    earlier = jnp.cumsum(onehot, axis=0) - onehot
    slot = jnp.sum(earlier * onehot, axis=1)
    return pair_ids * capacity + slot


def per_device(
    tokens,
    targets,
    token_weight,
    routes,
    router_weight,
    base_weight,
    direction_one,
    direction_two,
    filter_scale,
    landscape,
):
    tok_rows, feat = tokens.shape
    expert_count = router_weight.shape[1]
    width = base_weight.shape[2]
    own_hidden = base_weight.shape[3]
    dp_count = lax.axis_size("dp")
    mp_count = lax.axis_size("mp")
    mp_index = lax.axis_index("mp")

    def rebuilt(m, scale):
        return rebuild(base_weight[m, 0], direction_one[m, 0], direction_two[m, 0], scale[:, 0], landscape)

    gate_own = rebuild_call(0, base_weight, direction_one, direction_two, filter_scale, landscape)
    gate_left = shifted(gate_own, "mp", 1)
    gate_right = shifted(gate_own, "mp", -1)
    tokens_then, _ = lax.optimization_barrier((tokens, gate_own))

    flat_index = slot_target(routes, expert_count, CAP)
    placer = (
        flat_index[:, None] == jnp.arange(expert_count * CAP, dtype=jnp.int32)[None, :]
    ).astype(BF16)
    doubled = jnp.concatenate([tokens_then, tokens_then], axis=0)
    buffer = jnp.einsum("pk,pf->kf", placer, doubled, preferred_element_type=F32).astype(BF16)
    buffer = buffer.reshape(expert_count, CAP, feat)
    received = lax.all_to_all(buffer, EXPERT, split_axis=0, concat_axis=0, tiled=True)
    quarters = received.reshape(mp_count, (expert_count // mp_count) * CAP, feat)
    rows = quarters.shape[1]
    part = rows // 2

    scale_then, _ = lax.optimization_barrier((filter_scale, buffer))
    up_own, down_own = rebuilt(1, scale_then), rebuilt(2, scale_then)

    partial_logits = lax.dot_general(
        router_weight, tokens, (((0,), (1,)), ((), ())), preferred_element_type=F32
    )
    high = lax.reduce_precision(partial_logits, 8, 7)
    middle = lax.reduce_precision(partial_logits - high, 8, 7)
    low = partial_logits - high - middle
    wide = [matrix.astype(F32) for matrix in (gate_own, up_own, down_own)]
    energy = jnp.sum(jnp.sum(wide[0] ** 2, axis=0) * jnp.sum(wide[1] ** 2, axis=0))
    reach = jnp.max(jnp.sum(wide[2] ** 2, axis=1))
    longest = jnp.max(jnp.sum(received.astype(F32) ** 2, axis=2))
    kind = lax.broadcasted_iota(jnp.int32, high.shape, 0)
    limits = 1.02 * jnp.where(kind == 0, energy, jnp.where(kind == 1, reach, longest))
    extra = jnp.concatenate([high, middle, low, limits], axis=1).astype(BF16)
    head = extra.shape[0]

    pieces = []
    for step in range(mp_count):
        target = lax.rem(mp_index + step, mp_count)
        piece = lax.dynamic_index_in_dim(quarters, target, 0, keepdims=False)
        piece = jnp.concatenate([extra, piece], axis=0)
        pieces.append(shifted(piece, "mp", step) if step else piece)
    slots = jnp.concatenate(pieces, axis=1)

    up_then, down_then, _ = lax.optimization_barrier((up_own, down_own, received))
    up_left = shifted(up_then, "mp", 1)
    up_right = shifted(up_then, "mp", -1)
    down_left = shifted(down_then, "mp", 1)
    down_right = shifted(down_then, "mp", -1)
    gate_far = shifted(gate_left, "mp", 1)
    up_far = shifted(up_right, "mp", -1)

    forward = [slots]
    backward = [slots]
    for _ in range(1, dp_count // 2):
        forward.append(shifted(forward[-1], "dp", 1))
        backward.append(shifted(backward[-1], "dp", -1))
    far_low = shifted(forward[-1][: head + part], "dp", 1)
    far_high = shifted(backward[-1][head + part :], "dp", -1)

    middle_row = width // 2
    first_half, second_half, _, _ = lax.optimization_barrier((down_left, down_right, far_low, far_high))
    down_far = (
        shifted(first_half[:middle_row], "mp", 1), shifted(second_half[middle_row:], "mp", -1)
    )

    heads = [block[:head] for block in forward + backward[1:] + [far_low]]
    limits = functools.reduce(jnp.maximum, [block.astype(F32) for block in heads])
    limits = jnp.max(limits.reshape(head, mp_count, feat)[:, :, feat - tok_rows :], axis=(1, 2))
    devices = float(dp_count * mp_count)
    bound = 1.1 * devices * mp_count * limits[2] * jnp.sqrt(limits[0]) * jnp.sqrt(limits[1])
    bound = jnp.maximum(bound, 1e-20)
    to_wire = 32768.0 / bound
    from_wire = bound * (1.0 / 32768.0)

    parts = slots[:head].astype(F32).reshape(head, mp_count, 4, tok_rows)[:, :, :3]
    logits = jnp.sum(parts, axis=(1, 2))

    blocks = [slots]
    for ahead, behind in zip(forward[1:], backward[1:]):
        blocks += [ahead, behind]
    blocks += [far_low, far_high]
    skips = (head,) * (len(blocks) - 1) + (0,)
    all_rows = dp_count * rows
    slots_shape = jax.ShapeDtypeStruct((all_rows, width), BF16)
    total_shape = jax.ShapeDtypeStruct((all_rows, width), F32)
    place = mp_index.astype(jnp.int32).reshape(1)
    every, sums = expert_call(
        functools.partial(first_kernel, skips),
        (place, *blocks, gate_own, up_own, down_own),
        [slots_shape, total_shape], all_rows, width, own_hidden, 1,
    )
    sums = expert_call(
        middle_kernel,
        (every, sums, gate_left, up_left, down_left, gate_right, up_right, down_right),
        total_shape, all_rows, width, 2 * own_hidden, 0,
    )
    heights = [rows] * (dp_count - 1) + [part, part]
    hidden = expert_call(
        hidden_kernel, (every, gate_far, up_far),
        jax.ShapeDtypeStruct((all_rows, own_hidden), BF16), all_rows, width, 2 * own_hidden // 3, 0,
    )
    outs = expert_call(
        last_kernel,
        (hidden, sums, *down_far),
        [jax.ShapeDtypeStruct((height, width), F32) for height in heights],
        all_rows, width, own_hidden // 3, 0,
    )
    outs = [out * to_wire for out in outs]

    def both(below, above):
        pair = lax.optimization_barrier((below.astype(WIRE), above.astype(WIRE)))
        pair = lax.optimization_barrier((shifted(pair[0], "dp", -1), shifted(pair[1], "dp", 1)))
        return pair[0].astype(F32), pair[1].astype(F32)

    back, ahead = both(outs[-2], outs[-1])
    below, above = outs[-4], outs[-3]
    below = jnp.concatenate([below[:part] + back, below[part:]], axis=0)
    above = jnp.concatenate([above[:part], above[part:] + ahead], axis=0)
    back, ahead = both(below, above)
    for step in range(dp_count // 2 - 2, 0, -1):
        back, ahead = both(outs[2 * step - 1] + back, outs[2 * step] + ahead)
    result = ((outs[0] + back + ahead) * from_wire).astype(BF16)

    arrived = []
    for step in range(mp_count):
        target = lax.rem(mp_index + step, mp_count)
        piece = lax.dynamic_slice(result, (0, target * feat), (rows, feat))
        arrived.append(shifted(piece, "mp", step) if step else piece)

    def quarter(place):
        step = lax.rem(mp_index - place + mp_count, mp_count)
        chosen = arrived[-1]
        for i, piece in enumerate(arrived[:-1]):
            chosen = jnp.where(step == i, piece, chosen)
        return chosen

    expert_out = jnp.stack([quarter(i) for i in range(mp_count)]).reshape(expert_count, CAP, feat)
    returned = lax.all_to_all(expert_out, EXPERT, split_axis=0, concat_axis=0, tiled=True)

    expert_ids = jnp.arange(expert_count, dtype=jnp.int32)
    pick_first = jnp.sum(jnp.where(routes[:, 0][None, :] == expert_ids[:, None], logits, 0.0), axis=0)
    pick_second = jnp.sum(jnp.where(routes[:, 1][None, :] == expert_ids[:, None], logits, 0.0), axis=0)
    gate_first = 1.0 / (1.0 + jnp.exp(pick_second - pick_first))
    gate_second = 1.0 / (1.0 + jnp.exp(pick_first - pick_second))

    out_rows = returned.reshape(expert_count * CAP, feat)
    picked = jnp.dot(placer, out_rows, preferred_element_type=F32)
    first_out, second_out = picked[:tok_rows], picked[tok_rows:]
    combined = (
        tokens.astype(F32) + gate_first[:, None] * first_out + gate_second[:, None] * second_out
    )
    error = combined - targets.astype(F32)
    partial_loss = jnp.sum(token_weight[:, None] * error * error)
    loss_total = jnp.sum(to_all(partial_loss.reshape(1, 1), ("dp", "expert_0", "expert_1", "mp")))
    entries = tok_rows * dp_count * expert_count * feat * mp_count
    loss = (loss_total / entries).reshape(1)
    return (combined.astype(BF16), loss)


def solution(mesh):
    split = Mesh(
        mesh.devices.reshape(mesh.shape["dp"], 4, 2, mesh.shape["mp"]),
        ("dp", "expert_0", "expert_1", "mp"),
    )

    return jax.shard_map(
        per_device,
        mesh=split,
        in_specs=(
            P(DP_EXPERT, "mp"),
            P(DP_EXPERT, "mp"),
            P(DP_EXPERT),
            P(DP_EXPERT, None),
            P("mp", None),
            P(None, EXPERT, None, ("dp", "mp")),
            P(None, EXPERT, None, ("dp", "mp")),
            P(None, EXPERT, None, ("dp", "mp")),
            P(None, EXPERT, ("dp", "mp")),
            P(),
        ),
        out_specs=(P(DP_EXPERT, "mp"), P()),
        check_vma=False,
    )
```
